32 devices in a mesh: mem: 8 (over z, y), band: 4 (over x, core).
Axes of the slice: x: 2, y: 2, z: 4, core: 2. Of those that a mesh axis runs over, the one named last changes fastest.
Arguments:
- ensemble: float32 [256, 256, 256], P('mem', 'band'), may hold values from -8 to 8
- column_operator: float32 [128, 128], replicated, may hold values from -0.5 to 0.5
- patch_order: int32 [4, 64], P('band'), may hold values from 0 to 63, as said below
- obs_index: int32 [4, 64, 512], P('band'), may hold values from 0 to 255
- obs_count: int32 [4, 64], P('band', 'mem'), may hold values from 1 to 512
- obs_values: float32 [4, 64, 512], P('band', 'mem'), may hold values from -8 to 8
- obs_precision: float32 [4, 64, 512], P('band', 'mem'), may hold values from 2 to 50
Outputs:
- analysis: float32 [256, 256, 256], P('mem', 'band')
- transform: float32 [4, 64, 256, 256], P('band', 'mem')
The draws below stay inside these ranges and needn't reach their ends.
Inputs may be any that keep to these rules, and one draw needn't show every extreme that they name: `patch_order`: each row is a permutation of 0 to 63.
All inputs are finite; a program needn't handle non-finite values.
Results may differ from the reference program's by a relative error of at most 0.0003.
Values sent between devices are 32-bit elements; how exact they have to be, the bound alone decides.
A program may use at most 64 MiB of HBM per device.

```python
import math
import jax
import jax.numpy as jnp
from jax import lax

K = 256
LEV = 128
NCH = 128
PCOLS = 2
OBS = 512
ITERS = 12
BAND_PATCHES = 64
NPATCH = 256
PC = 256
CAND = 256
N_BAND = 4


def draw_patch_order(key, part):
    keys = jax.random.split(jax.random.fold_in(key, 11), N_BAND)
    return jax.vmap(lambda single: jax.random.permutation(single, BAND_PATCHES))(keys).astype(jnp.int32)


def draw_obs_count(key, part):
    first, second, third = jax.random.split(jax.random.fold_in(key, 23), 3)
    total = N_BAND * BAND_PATCHES
    top_power = OBS.bit_length() - 1
    powers = jax.random.randint(first, (total,), 0, top_power).astype(jnp.int32)
    lowest = jnp.left_shift(jnp.ones((total,), jnp.int32), powers)
    counts = lowest + jax.random.randint(second, (total,), 0, lowest).astype(jnp.int32)
    spot = jax.random.randint(third, (), 0, total)
    places = jnp.arange(total, dtype=jnp.int32)
    counts = jnp.where(places == spot, OBS, counts)
    counts = jnp.where(places == (spot + 1) % total, 1, counts)
    return counts.reshape(N_BAND, BAND_PATCHES).astype(jnp.int32)


def touch_ends(drawn, key, low, high):
    longest = drawn.shape.index(max(drawn.shape))
    spots = []
    for shift in (0, 1):
        where = [jax.random.randint(jax.random.fold_in(key, axis), (), 0, length) for axis, length in enumerate(drawn.shape)]
        where[longest] = (where[longest] + shift) % drawn.shape[longest]
        spots.append(tuple(where))
    return drawn.at[spots[0]].set(low).at[spots[1]].set(high)


def steps_of(rng, dims, shards, smallest, top_value):
    def one(axis_at, shards_of):
        draws = jax.random.uniform(jax.random.fold_in(jax.random.fold_in(rng, 6), axis_at), (shards_of,), jnp.float32, smallest / len(shards), top_value / len(shards))
        return jnp.repeat(jnp.exp(draws), dims[axis_at] // shards_of).reshape((-1,) + (1,) * (len(dims) - axis_at - 1))

    loudness = one(*shards[0])
    for cut in shards[1:]:
        loudness = loudness * one(*cut)
    return loudness


def gaussian(key, shape, deviation, limit, pieces=(), kind=jnp.bfloat16):
    values = jax.random.normal(key, shape, jnp.float32) * deviation
    if len(pieces) > 0:
        values = steps_of(key, shape, pieces, -0.22, 0.18) * values
    return jnp.clip(values, min=-limit, max=limit).astype(kind)


def setup_inputs(seed: int = 0) -> dict:
    key_of = jax.random.split(jax.random.key(seed), 8)
    ensemble = gaussian(key_of[0], (K, NPATCH, PC), 2.5, 8.0, ((0, 8), (1, 4)), jnp.float32)
    column_operator = jnp.clip(jax.random.uniform(key_of[1], (LEV, NCH), jnp.float32, -0.5, 0.5), -0.5, 0.5)
    patch_order = draw_patch_order(jax.random.fold_in(key_of[7], 71), 0)
    obs_index = touch_ends(jax.random.randint(key_of[3], (N_BAND, BAND_PATCHES, OBS), 0, CAND), jax.random.fold_in(key_of[3], 1), 0, CAND - 1).astype(jnp.int32)
    obs_count = draw_obs_count(jax.random.fold_in(key_of[7], 71), 0)
    obs_values = gaussian(key_of[5], (N_BAND, BAND_PATCHES, OBS), 1.5, 8.0, ((0, 4), (1, 8)), jnp.float32)
    obs_precision = jnp.clip(jnp.exp(math.log(50.0) - 3.218876 * jax.random.uniform(key_of[6], (N_BAND, BAND_PATCHES, OBS), jnp.float32) ** steps_of(key_of[6], (N_BAND, BAND_PATCHES, OBS), ((0, 4), (1, 8)), -0.2, 0.2)), 2.0, 50.0)
    return {"ensemble": ensemble, "column_operator": column_operator, "patch_order": patch_order, "obs_index": obs_index, "obs_count": obs_count, "obs_values": obs_values, "obs_precision": obs_precision}


def analyse(members, column_operator, index, count, values, precision):
    highest = lax.Precision.HIGHEST
    rows = members.shape[0]
    channel_values = jnp.dot(members.reshape(rows * PCOLS, LEV), column_operator, precision=highest).reshape(rows, PCOLS * NCH)
    picks = jnp.broadcast_to(index[None, :], (rows, OBS))
    observed = jnp.take_along_axis(channel_values, picks, axis=1)
    live = (jnp.arange(OBS, dtype=jnp.int32) < count).astype(jnp.float32)
    obs_weight = precision * live
    state_mean = lax.optimization_barrier(jnp.mean(members, axis=0))
    state_pert = members - state_mean
    obs_mean = lax.optimization_barrier(jnp.mean(observed, axis=0))
    obs_pert = observed - obs_mean
    innov = (values - obs_mean) * obs_weight
    gram = jnp.dot(obs_pert * obs_weight, obs_pert.T, precision=highest)
    identity = jnp.eye(rows, dtype=jnp.float32)
    system = gram + (K - 1.0) * identity
    trace_value = jnp.trace(system)
    ymat = system / trace_value
    zmat = identity
    for sweep in range(ITERS):
        turn = 1.5 * identity - 0.5 * jnp.dot(zmat, ymat, precision=highest)
        ymat, zmat = (jnp.dot(ymat, turn, precision=highest), jnp.dot(turn, zmat, precision=highest))
    root = zmat / jnp.sqrt(trace_value)
    spread = math.sqrt(K - 1.0) * root
    projected = jnp.dot(obs_pert, innov, precision=highest)
    mean_weight = jnp.dot(root, jnp.dot(root, projected, precision=highest), precision=highest)
    coef = spread + mean_weight[:, None]
    result = state_mean + jnp.dot(coef.T, state_pert, precision=highest)
    return (spread, result)

def reference(ensemble, column_operator, patch_order, obs_index, obs_count, obs_values, obs_precision):
    bands = jnp.repeat(jnp.arange(N_BAND, dtype=jnp.int32), BAND_PATCHES)
    patch_ids = (bands * BAND_PATCHES + patch_order.reshape(-1)).astype(jnp.int32)

    def one(items):
        pid, index, count, values, precision = items
        members = lax.dynamic_index_in_dim(ensemble, pid, 1, keepdims=False)
        return analyse(members, column_operator, index, count, values, precision)
    spreads, results = lax.map(one, (patch_ids, obs_index.reshape(-1, OBS), obs_count.reshape(-1), obs_values.reshape(-1, OBS), obs_precision.reshape(-1, OBS)))
    analysis = jnp.zeros_like(ensemble).at[:, patch_ids, :].set(jnp.swapaxes(results, 0, 1))
    transform = spreads.reshape(N_BAND, BAND_PATCHES, K, K)
    return (analysis, transform)
```

```python
import functools
import math

import jax
import jax.numpy as jnp
from jax import lax
from jax.experimental import pallas as pl
from jax.experimental.pallas import tpu as pltpu
from jax.sharding import PartitionSpec as P

ITERS = 12
LIGHT = 8
MESH = pl.DeviceIdType.MESH
HIGHEST = lax.Precision.HIGHEST


def whole():
    return pl.BlockSpec(memory_space=pltpu.VMEM)


def pieces(x):
    high = x.astype(jnp.bfloat16)
    return high, (x - high.astype(jnp.float32)).astype(jnp.bfloat16)


def product(left, right, full, right_dim=0):
    lh, ll = left
    rh, rl = right
    lefts = [lh, lh, ll, ll] if full else [lh, lh, ll]
    rights = [rh, rl, rh, rl] if full else [rh, rl, rh]
    return lax.dot_general(
        jnp.concatenate(lefts, axis=1),
        jnp.concatenate(rights, axis=right_dim),
        (((1,), (right_dim,)), ((), ())),
        preferred_element_type=jnp.float32,
    )


def exact(left, right, right_dim=0):
    return lax.dot_general(
        left, right, (((1,), (right_dim,)), ((), ())),
        precision=HIGHEST, preferred_element_type=jnp.float32,
    )


def sweep(y_ref, z_ref, group, full, last):
    for g in range(group):
        y, z = y_ref[g], z_ref[g]
        yp, zp = pieces(y), pieces(z)
        turn = pieces(product(zp, yp, full))
        if not last:
            y_ref[g] = 1.5 * y - 0.5 * product(yp, turn, full)
        z_ref[g] = 1.5 * z - 0.5 * product(turn, zp, full)


def partner(me, d, n_mem):
    if n_mem % 2:
        return lax.rem(me + d + 1, n_mem)
    half = n_mem // 2
    side = me // half
    across = (1 - side) * half + lax.rem(me + d, half)
    near = side * half + lax.rem(me + d + 1, half)
    return jnp.where(d < half, across, near)


def analyse(n_mem, group, order_hbm, count_hbm, x_hbm, op_hbm, index_hbm, value_hbm, weight_hbm, spread_out, back_ref,
            order_ref, count_ref, op_ref, index_ref, value_ref, weight_ref, spread_ref,
            lanes_ref, sends_ref, inbox, outbox, pert_ref, y_ref, z_ref, col_ref, mean_ref,
            load_sem, lane_sem, spread_sem, in_send, in_recv, own_sem, out_send, out_recv, home_sem):
    per_worker, workers, rows_dev, cells = inbox.shape
    members = workers * rows_dev
    levels = op_ref.shape[0]
    slots = index_ref.shape[1]
    me = lax.axis_index("mem")
    halves, _, lanes = lanes_ref.shape
    band = order_ref.shape[0]
    barrier = pltpu.get_barrier_semaphore()

    order_load = pltpu.make_async_copy(order_hbm, order_ref, load_sem.at[0])
    order_load.start()
    lane_loads = [
        pltpu.make_async_copy(x_hbm.at[:, pl.ds(h * lanes, lanes)], lanes_ref.at[h], lane_sem.at[h])
        for h in range(halves)
    ]
    for load in lane_loads:
        load.start()

    def greet(d, carry):
        pl.semaphore_signal(barrier, inc=1, device_id={"mem": partner(me, d, n_mem)}, device_id_type=MESH)
        return carry

    lax.fori_loop(0, n_mem - 1, greet, 0)
    mine = pl.ds(pl.multiple_of(me * per_worker, per_worker), per_worker)
    loads = [
        pltpu.make_async_copy(source, target, load_sem.at[1 + n])
        for n, (source, target) in enumerate([
            (count_hbm, count_ref), (op_hbm, op_ref), (index_hbm.at[mine], index_ref),
            (value_hbm, value_ref), (weight_hbm, weight_ref),
        ])
    ]
    for load in loads:
        load.start()
    order_load.wait()
    for load in lane_loads:
        load.wait()

    def stage(i):
        def one(w, carry):
            q = order_ref[w * per_worker + i]
            for h in range(halves):
                sends_ref[w, i, :, h * lanes:(h + 1) * lanes] = lanes_ref[h, pl.ds(q, rows_dev, stride=band), :]
            return carry

        lax.fori_loop(0, n_mem, one, 0)

    stage(0)
    pl.semaphore_wait(barrier, n_mem - 1)

    def keep(i):
        return pltpu.make_async_copy(spread_ref.at[i], spread_out.at[i], spread_sem.at[i])

    def own_in(i):
        return pltpu.make_async_copy(sends_ref.at[me, i], inbox.at[i, me], own_sem.at[i])

    def own_back(i):
        return pltpu.make_async_copy(outbox.at[i, me], back_ref.at[me, i], home_sem.at[i])

    def issue(i):
        own_in(i).start()

        def one(d, carry):
            peer = partner(me, d, n_mem)
            pltpu.make_async_remote_copy(
                src_ref=sends_ref.at[peer, i], dst_ref=inbox.at[i, me],
                send_sem=in_send, recv_sem=in_recv.at[i],
                device_id={"mem": peer}, device_id_type=MESH,
            ).start()
            return carry

        lax.fori_loop(0, n_mem - 1, one, 0)

    def feed(i, carry):
        stage(i)
        issue(i)
        return carry

    issue(0)
    lax.fori_loop(1, per_worker, feed, 0)
    for load in loads:
        load.wait()
    eye = (
        lax.broadcasted_iota(jnp.int32, (members, members), 0)
        == lax.broadcasted_iota(jnp.int32, (members, members), 1)
    )

    def run(base, size):
        for g in range(size):
            own_in(base + g).wait()
            arrived = inbox.at[base + g, pl.ds(0, n_mem - 1)]
            pltpu.make_async_copy(arrived, arrived, in_recv.at[base + g]).wait()
        scales = [prepare(base + g, g) for g in range(size)]

        def light(k, carry):
            sweep(y_ref, z_ref, size, False, False)
            return carry

        def firm(k, carry):
            sweep(y_ref, z_ref, size, True, False)
            return carry

        lax.fori_loop(1, LIGHT, light, 0)
        lax.fori_loop(LIGHT, ITERS - 1, firm, 0)
        sweep(y_ref, z_ref, size, True, True)
        for g in range(size):
            finish(base + g, g, scales[g])
            launch(base + g)

    def launch(spot):
        own_back(spot).start()

        def one(d, carry):
            peer = partner(me, d, n_mem)
            pltpu.make_async_remote_copy(
                src_ref=outbox.at[spot, peer], dst_ref=back_ref.at[me, spot],
                send_sem=out_send, recv_sem=out_recv,
                device_id={"mem": peer}, device_id_type=MESH,
            ).start()
            return carry

        lax.fori_loop(0, n_mem - 1, one, 0)

    def prepare(spot, g):
        state = inbox[spot].reshape(members, cells)
        mean = jnp.mean(state, axis=0, keepdims=True)
        pert = state - mean
        pert_ref[g] = pert
        op = op_ref[...]
        columns = cells // levels
        op_pieces = pieces(op)
        chan = jnp.concatenate([product(pieces(pert[:, c * levels:(c + 1) * levels]), op_pieces, False) for c in range(columns)], axis=1)
        wide = jnp.broadcast_to(mean, (8, cells))
        chan_mean = jnp.concatenate([exact(wide[:, c * levels:(c + 1) * levels], op) for c in range(columns)], axis=1)
        width = chan.shape[1]
        index = index_ref[pl.ds(spot, 1), :]
        live = lax.broadcasted_iota(jnp.int32, (1, slots), 1) < count_ref[spot]
        weight = jnp.where(live, weight_ref[pl.ds(spot, 1), :], 0.0)
        value = weight * value_ref[pl.ds(spot, 1), :]
        picker = (lax.broadcasted_iota(jnp.int32, (width, slots), 0) == index).astype(jnp.bfloat16)
        sub = lax.broadcasted_iota(jnp.int32, (16, slots), 0)
        stack = jnp.where(sub == 0, weight, jnp.where(sub == 1, value, 0.0))
        s0 = stack.astype(jnp.bfloat16)
        left = stack - s0.astype(jnp.float32)
        s1 = left.astype(jnp.bfloat16)
        s2 = (left - s1.astype(jnp.float32)).astype(jnp.bfloat16)
        binned = lax.dot_general(
            jnp.concatenate([s0, s1, s2], axis=0), picker, (((1,), (1,)), ((), ())),
            preferred_element_type=jnp.float32,
        )
        binned = binned[0:16] + (binned[16:32] + binned[32:48])
        total = binned[0:1]
        innov = binned[1:2] - chan_mean[0:1] * total
        system = exact(chan * total, chan, 1) + jnp.where(eye, members - 1.0, 0.0)
        col_ref[g] = jnp.sum(chan * innov, axis=1, keepdims=True)
        mean_ref[g] = wide
        trace_value = jnp.sum(jnp.sum(jnp.where(eye, system, 0.0), axis=0, keepdims=True), axis=1, keepdims=True)
        y = system / trace_value
        yp = pieces(y)
        z_ref[g] = jnp.where(eye, 1.5, 0.0) - 0.5 * y
        y_ref[g] = 1.5 * y - 0.5 * product(yp, yp, False)
        return trace_value

    def finish(spot, g, trace_value):
        z = z_ref[g]
        spread = z * (math.sqrt(members - 1.0) / jnp.sqrt(trace_value))
        spread_ref[spot] = spread
        keep(spot).start()
        inner = jnp.sum(z * col_ref[g], axis=0, keepdims=True)
        weights = jnp.sum(z * inner, axis=1, keepdims=True) / trace_value
        pert = pert_ref[g]
        shift = mean_ref[g][0:1] + jnp.sum(pert * weights, axis=0, keepdims=True)
        update = shift + product(pieces(spread), pieces(pert), False)
        outbox[spot] = update.reshape(workers, rows_dev, cells)

    edge = 1 if group > 1 and per_worker % group == 0 and per_worker > group else 0
    middle = (per_worker - 2 * edge) // group

    def step(t, carry):
        run(edge + t * group, group)
        return carry

    if edge:
        run(0, 1)
    lax.fori_loop(0, middle, step, 0)
    if edge:
        run(per_worker - 1, 1)
    sent = sends_ref.at[pl.ds(0, n_mem - 1)]
    pltpu.make_async_copy(sent, sent, in_send).wait()
    posted = back_ref.at[pl.ds(0, n_mem - 1)]
    pltpu.make_async_copy(posted, posted, out_send).wait()
    pltpu.make_async_copy(posted, posted, out_recv).wait()
    for i in range(per_worker):
        own_back(i).wait()
        keep(i).wait()


def restore(order_hbm, back, spread, out, spread_out, order_ref, order_sem, spread_sem, sem):
    n_mem, per_worker = back.shape[:2]
    load = pltpu.make_async_copy(order_hbm, order_ref, order_sem)
    load.start()
    passed = pltpu.make_async_copy(spread, spread_out, spread_sem)
    passed.start()
    load.wait()

    def place(t, carry):
        pltpu.make_async_copy(
            back.at[t // per_worker, lax.rem(t, per_worker)], out.at[:, order_ref[t], :], sem
        ).start()
        return carry

    lax.fori_loop(0, n_mem * per_worker, place, 0, unroll=8)
    pltpu.make_async_copy(out, out, sem).wait()
    passed.wait()


def local(ensemble, column_operator, patch_order, obs_index, obs_count, obs_values, obs_precision):
    rows_dev, band, cells = ensemble.shape
    slots = obs_index.shape[2]
    n_mem = lax.axis_size("mem")
    per_worker = band // n_mem
    members = rows_dev * n_mem
    group = 2 if per_worker % 2 == 0 else 1
    order = patch_order[0]
    held = pl.BlockSpec(memory_space=pltpu.HBM)
    free = pl.BlockSpec(memory_space=pl.ANY)
    block = jax.ShapeDtypeStruct((n_mem, per_worker, rows_dev, cells), jnp.float32)
    squares = jax.ShapeDtypeStruct((per_worker, members, members), jnp.float32)

    spread, back = pl.pallas_call(
        functools.partial(analyse, n_mem, group),
        out_shape=[squares, block],
        in_specs=[held] * 7,
        out_specs=[free, free],
        scratch_shapes=[
            pltpu.SMEM((band,), jnp.int32),
            pltpu.SMEM((per_worker,), jnp.int32),
            pltpu.VMEM(column_operator.shape, jnp.float32),
            pltpu.VMEM((per_worker, slots), jnp.int32),
            pltpu.VMEM((per_worker, slots), jnp.float32),
            pltpu.VMEM((per_worker, slots), jnp.float32),
            pltpu.VMEM((per_worker, members, members), jnp.float32),
            pltpu.VMEM((cells // 128, rows_dev * band, 128), jnp.float32),
            pltpu.VMEM((n_mem, per_worker, rows_dev, cells), jnp.float32),
            pltpu.VMEM((per_worker, n_mem, rows_dev, cells), jnp.float32),
            pltpu.VMEM((per_worker, n_mem, rows_dev, cells), jnp.float32),
            pltpu.VMEM((group, members, cells), jnp.float32),
            pltpu.VMEM((group, members, members), jnp.float32),
            pltpu.VMEM((group, members, members), jnp.float32),
            pltpu.VMEM((group, members, 1), jnp.float32),
            pltpu.VMEM((group, 8, cells), jnp.float32),
            pltpu.SemaphoreType.DMA((6,)),
            pltpu.SemaphoreType.DMA((cells // 128,)),
            pltpu.SemaphoreType.DMA((per_worker,)),
            pltpu.SemaphoreType.DMA(()),
            pltpu.SemaphoreType.DMA((per_worker,)),
            pltpu.SemaphoreType.DMA((per_worker,)),
            pltpu.SemaphoreType.DMA(()),
            pltpu.SemaphoreType.DMA(()),
            pltpu.SemaphoreType.DMA((per_worker,)),
        ],
        compiler_params=pltpu.CompilerParams(collective_id=0, has_side_effects=True, vmem_limit_bytes=40 << 20),
        name="analyse",
    )(*[pltpu.with_memory_space_constraint(part, pltpu.HBM) for part in (order, obs_count[0], ensemble.reshape(rows_dev * band, cells), column_operator, obs_index[0], obs_values[0], obs_precision[0])])

    restored, transform = pl.pallas_call(
        restore,
        out_shape=[jax.ShapeDtypeStruct((rows_dev, band, cells), jnp.float32), squares],
        in_specs=[held, free, free],
        out_specs=[held, held],
        scratch_shapes=[
            pltpu.SMEM((band,), jnp.int32),
            pltpu.SemaphoreType.DMA(()),
            pltpu.SemaphoreType.DMA(()),
            pltpu.SemaphoreType.DMA(()),
        ],
        compiler_params=pltpu.CompilerParams(vmem_limit_bytes=16 << 20),
        name="restore_patches",
    )(order, back, spread)
    return (restored, transform[None])


def solution(mesh):
    placed = (
        P("mem", "band", None),
        P(),
        P("band", None),
        P("band", None, None),
        P("band", "mem"),
        P("band", "mem", None),
        P("band", "mem", None),
    )
    return jax.shard_map(
        local,
        mesh=mesh,
        in_specs=placed,
        out_specs=(P("mem", "band", None), P("band", "mem", None, None)),
        check_vma=False,
    )
```

```python
import functools
import math

import jax
import jax.numpy as jnp
from jax import lax
from jax.experimental import pallas as pl
from jax.experimental.pallas import tpu as pltpu
from jax.sharding import PartitionSpec as P

ITERS = 12
LIGHT = 8
MESH = pl.DeviceIdType.MESH
HIGHEST = lax.Precision.HIGHEST


def whole():
    return pl.BlockSpec(memory_space=pltpu.VMEM)


def pieces(x):
    high = x.astype(jnp.bfloat16)
    return high, (x - high.astype(jnp.float32)).astype(jnp.bfloat16)


def product(left, right, full, right_dim=0):
    lh, ll = left
    rh, rl = right
    lefts = [lh, lh, ll, ll] if full else [lh, lh, ll]
    rights = [rh, rl, rh, rl] if full else [rh, rl, rh]
    return lax.dot_general(
        jnp.concatenate(lefts, axis=1),
        jnp.concatenate(rights, axis=right_dim),
        (((1,), (right_dim,)), ((), ())),
        preferred_element_type=jnp.float32,
    )


def exact(left, right, right_dim=0):
    return lax.dot_general(
        left, right, (((1,), (right_dim,)), ((), ())),
        precision=HIGHEST, preferred_element_type=jnp.float32,
    )


def sweep(y_ref, z_ref, group, full, last):
    for g in range(group):
        y, z = y_ref[g], z_ref[g]
        yp, zp = pieces(y), pieces(z)
        turn = pieces(product(zp, yp, full))
        if not last:
            y_ref[g] = 1.5 * y - 0.5 * product(yp, turn, full)
        z_ref[g] = 1.5 * z - 0.5 * product(turn, zp, full)


def partner(me, d, n_mem):
    return lax.rem(me + d + 1, n_mem)


def analyse(n_mem, group, order_hbm, count_hbm, x_hbm, op_hbm, index_hbm, value_hbm, weight_hbm, spread_out, back_ref,
            order_ref, count_ref, op_ref, index_ref, value_ref, weight_ref, spread_ref,
            lanes_ref, sends_ref, inbox, outbox, pert_ref, y_ref, z_ref, col_ref, mean_ref,
            load_sem, lane_sem, spread_sem, in_send, in_recv, own_sem, out_send, out_recv, home_sem):
    per_worker, workers, rows_dev, cells = inbox.shape
    members = workers * rows_dev
    levels = op_ref.shape[0]
    slots = index_ref.shape[1]
    me = lax.axis_index("mem")
    halves, _, lanes = lanes_ref.shape
    band = order_ref.shape[0]
    barrier = pltpu.get_barrier_semaphore()

    order_load = pltpu.make_async_copy(order_hbm, order_ref, load_sem.at[0])
    order_load.start()
    lane_loads = [
        pltpu.make_async_copy(x_hbm.at[:, pl.ds(h * lanes, lanes)], lanes_ref.at[h], lane_sem.at[h])
        for h in range(halves)
    ]
    for load in lane_loads:
        load.start()

    def greet(d, carry):
        pl.semaphore_signal(barrier, inc=1, device_id={"mem": partner(me, d, n_mem)}, device_id_type=MESH)
        return carry

    lax.fori_loop(0, n_mem - 1, greet, 0)
    mine = pl.ds(pl.multiple_of(me * per_worker, per_worker), per_worker)
    loads = [
        pltpu.make_async_copy(source, target, load_sem.at[1 + n])
        for n, (source, target) in enumerate([
            (count_hbm, count_ref), (op_hbm, op_ref), (index_hbm.at[mine], index_ref),
            (value_hbm, value_ref), (weight_hbm, weight_ref),
        ])
    ]
    for load in loads:
        load.start()
    order_load.wait()
    for load in lane_loads:
        load.wait()

    def stage(i):
        def one(w, carry):
            q = order_ref[w * per_worker + i]
            for h in range(halves):
                sends_ref[w, i, :, h * lanes:(h + 1) * lanes] = lanes_ref[h, pl.ds(q, rows_dev, stride=band), :]
            return carry

        lax.fori_loop(0, n_mem, one, 0)

    stage(0)
    pl.semaphore_wait(barrier, n_mem - 1)

    def keep(i):
        return pltpu.make_async_copy(spread_ref.at[i], spread_out.at[i], spread_sem.at[i])

    def own_in(i):
        return pltpu.make_async_copy(sends_ref.at[me, i], inbox.at[i, me], own_sem.at[i])

    def own_back(i):
        return pltpu.make_async_copy(outbox.at[i, me], back_ref.at[me, i], home_sem.at[i])

    def issue(i):
        own_in(i).start()

        def one(d, carry):
            peer = partner(me, d, n_mem)
            pltpu.make_async_remote_copy(
                src_ref=sends_ref.at[peer, i], dst_ref=inbox.at[i, me],
                send_sem=in_send, recv_sem=in_recv.at[i],
                device_id={"mem": peer}, device_id_type=MESH,
            ).start()
            return carry

        lax.fori_loop(0, n_mem - 1, one, 0)

    def feed(i, carry):
        stage(i)
        issue(i)
        return carry

    issue(0)
    lax.fori_loop(1, per_worker, feed, 0)
    for load in loads:
        load.wait()
    eye = (
        lax.broadcasted_iota(jnp.int32, (members, members), 0)
        == lax.broadcasted_iota(jnp.int32, (members, members), 1)
    )

    def run(base, size):
        for g in range(size):
            own_in(base + g).wait()
            arrived = inbox.at[base + g, pl.ds(0, n_mem - 1)]
            pltpu.make_async_copy(arrived, arrived, in_recv.at[base + g]).wait()
        scales = [prepare(base + g, g) for g in range(size)]

        def light(k, carry):
            sweep(y_ref, z_ref, size, False, False)
            return carry

        def firm(k, carry):
            sweep(y_ref, z_ref, size, True, False)
            return carry

        lax.fori_loop(1, LIGHT, light, 0)
        lax.fori_loop(LIGHT, ITERS - 1, firm, 0)
        sweep(y_ref, z_ref, size, True, True)
        for g in range(size):
            finish(base + g, g, scales[g])
            launch(base + g)

    def launch(spot):
        own_back(spot).start()

        def one(d, carry):
            peer = partner(me, d, n_mem)
            pltpu.make_async_remote_copy(
                src_ref=outbox.at[spot, peer], dst_ref=back_ref.at[me, spot],
                send_sem=out_send, recv_sem=out_recv,
                device_id={"mem": peer}, device_id_type=MESH,
            ).start()
            return carry

        lax.fori_loop(0, n_mem - 1, one, 0)

    def prepare(spot, g):
        state = inbox[spot].reshape(members, cells)
        mean = jnp.mean(state, axis=0, keepdims=True)
        pert = state - mean
        pert_ref[g] = pert
        op = op_ref[...]
        columns = cells // levels
        op_pieces = pieces(op)
        chan = jnp.concatenate([product(pieces(pert[:, c * levels:(c + 1) * levels]), op_pieces, False) for c in range(columns)], axis=1)
        wide = jnp.broadcast_to(mean, (8, cells))
        chan_mean = jnp.concatenate([exact(wide[:, c * levels:(c + 1) * levels], op) for c in range(columns)], axis=1)
        width = chan.shape[1]
        index = index_ref[pl.ds(spot, 1), :]
        live = lax.broadcasted_iota(jnp.int32, (1, slots), 1) < count_ref[spot]
        weight = jnp.where(live, weight_ref[pl.ds(spot, 1), :], 0.0)
        value = weight * value_ref[pl.ds(spot, 1), :]
        picker = (lax.broadcasted_iota(jnp.int32, (width, slots), 0) == index).astype(jnp.bfloat16)
        sub = lax.broadcasted_iota(jnp.int32, (16, slots), 0)
        stack = jnp.where(sub == 0, weight, jnp.where(sub == 1, value, 0.0))
        s0 = stack.astype(jnp.bfloat16)
        left = stack - s0.astype(jnp.float32)
        s1 = left.astype(jnp.bfloat16)
        s2 = (left - s1.astype(jnp.float32)).astype(jnp.bfloat16)
        binned = lax.dot_general(
            jnp.concatenate([s0, s1, s2], axis=0), picker, (((1,), (1,)), ((), ())),
            preferred_element_type=jnp.float32,
        )
        binned = binned[0:16] + (binned[16:32] + binned[32:48])
        total = binned[0:1]
        innov = binned[1:2] - chan_mean[0:1] * total
        system = exact(chan * total, chan, 1) + jnp.where(eye, members - 1.0, 0.0)
        col_ref[g] = jnp.sum(chan * innov, axis=1, keepdims=True)
        mean_ref[g] = wide
        trace_value = jnp.sum(jnp.sum(jnp.where(eye, system, 0.0), axis=0, keepdims=True), axis=1, keepdims=True)
        y = system / trace_value
        yp = pieces(y)
        z_ref[g] = jnp.where(eye, 1.5, 0.0) - 0.5 * y
        y_ref[g] = 1.5 * y - 0.5 * product(yp, yp, False)
        return trace_value

    def finish(spot, g, trace_value):
        z = z_ref[g]
        spread = z * (math.sqrt(members - 1.0) / jnp.sqrt(trace_value))
        spread_ref[spot] = spread
        keep(spot).start()
        inner = jnp.sum(z * col_ref[g], axis=0, keepdims=True)
        weights = jnp.sum(z * inner, axis=1, keepdims=True) / trace_value
        pert = pert_ref[g]
        shift = mean_ref[g][0:1] + jnp.sum(pert * weights, axis=0, keepdims=True)
        update = shift + product(pieces(spread), pieces(pert), False)
        outbox[spot] = update.reshape(workers, rows_dev, cells)

    edge = 1 if group > 1 and per_worker % group == 0 and per_worker > group else 0
    middle = (per_worker - 2 * edge) // group

    def step(t, carry):
        run(edge + t * group, group)
        return carry

    if edge:
        run(0, 1)
    lax.fori_loop(0, middle, step, 0)
    if edge:
        run(per_worker - 1, 1)
    sent = sends_ref.at[pl.ds(0, n_mem - 1)]
    pltpu.make_async_copy(sent, sent, in_send).wait()
    posted = back_ref.at[pl.ds(0, n_mem - 1)]
    pltpu.make_async_copy(posted, posted, out_send).wait()
    pltpu.make_async_copy(posted, posted, out_recv).wait()
    for i in range(per_worker):
        own_back(i).wait()
        keep(i).wait()


def restore(order_hbm, back, spread, out, spread_out, order_ref, order_sem, spread_sem, sem):
    n_mem, per_worker = back.shape[:2]
    load = pltpu.make_async_copy(order_hbm, order_ref, order_sem)
    load.start()
    passed = pltpu.make_async_copy(spread, spread_out, spread_sem)
    passed.start()
    load.wait()

    def place(t, carry):
        pltpu.make_async_copy(
            back.at[t // per_worker, lax.rem(t, per_worker)], out.at[:, order_ref[t], :], sem
        ).start()
        return carry

    lax.fori_loop(0, n_mem * per_worker, place, 0, unroll=8)
    pltpu.make_async_copy(out, out, sem).wait()
    passed.wait()


def local(ensemble, column_operator, patch_order, obs_index, obs_count, obs_values, obs_precision):
    rows_dev, band, cells = ensemble.shape
    slots = obs_index.shape[2]
    n_mem = lax.axis_size("mem")
    per_worker = band // n_mem
    members = rows_dev * n_mem
    group = 2 if per_worker % 2 == 0 else 1
    order = patch_order[0]
    held = pl.BlockSpec(memory_space=pltpu.HBM)
    free = pl.BlockSpec(memory_space=pl.ANY)
    block = jax.ShapeDtypeStruct((n_mem, per_worker, rows_dev, cells), jnp.float32)
    squares = jax.ShapeDtypeStruct((per_worker, members, members), jnp.float32)

    spread, back = pl.pallas_call(
        functools.partial(analyse, n_mem, group),
        out_shape=[squares, block],
        in_specs=[held] * 7,
        out_specs=[free, free],
        scratch_shapes=[
            pltpu.SMEM((band,), jnp.int32),
            pltpu.SMEM((per_worker,), jnp.int32),
            pltpu.VMEM(column_operator.shape, jnp.float32),
            pltpu.VMEM((per_worker, slots), jnp.int32),
            pltpu.VMEM((per_worker, slots), jnp.float32),
            pltpu.VMEM((per_worker, slots), jnp.float32),
            pltpu.VMEM((per_worker, members, members), jnp.float32),
            pltpu.VMEM((cells // 128, rows_dev * band, 128), jnp.float32),
            pltpu.VMEM((n_mem, per_worker, rows_dev, cells), jnp.float32),
            pltpu.VMEM((per_worker, n_mem, rows_dev, cells), jnp.float32),
            pltpu.VMEM((per_worker, n_mem, rows_dev, cells), jnp.float32),
            pltpu.VMEM((group, members, cells), jnp.float32),
            pltpu.VMEM((group, members, members), jnp.float32),
            pltpu.VMEM((group, members, members), jnp.float32),
            pltpu.VMEM((group, members, 1), jnp.float32),
            pltpu.VMEM((group, 8, cells), jnp.float32),
            pltpu.SemaphoreType.DMA((6,)),
            pltpu.SemaphoreType.DMA((cells // 128,)),
            pltpu.SemaphoreType.DMA((per_worker,)),
            pltpu.SemaphoreType.DMA(()),
            pltpu.SemaphoreType.DMA((per_worker,)),
            pltpu.SemaphoreType.DMA((per_worker,)),
            pltpu.SemaphoreType.DMA(()),
            pltpu.SemaphoreType.DMA(()),
            pltpu.SemaphoreType.DMA((per_worker,)),
        ],
        compiler_params=pltpu.CompilerParams(collective_id=0, has_side_effects=True, vmem_limit_bytes=40 << 20),
        name="analyse",
    )(*[pltpu.with_memory_space_constraint(part, pltpu.HBM) for part in (order, obs_count[0], ensemble.reshape(rows_dev * band, cells), column_operator, obs_index[0], obs_values[0], obs_precision[0])])

    restored, transform = pl.pallas_call(
        restore,
        out_shape=[jax.ShapeDtypeStruct((rows_dev, band, cells), jnp.float32), squares],
        in_specs=[held, free, free],
        out_specs=[held, held],
        scratch_shapes=[
            pltpu.SMEM((band,), jnp.int32),
            pltpu.SemaphoreType.DMA(()),
            pltpu.SemaphoreType.DMA(()),
            pltpu.SemaphoreType.DMA(()),
        ],
        compiler_params=pltpu.CompilerParams(vmem_limit_bytes=16 << 20),
        name="restore_patches",
    )(order, back, spread)
    return (restored, transform[None])


def solution(mesh):
    placed = (
        P("mem", "band", None),
        P(),
        P("band", None),
        P("band", None, None),
        P("band", "mem"),
        P("band", "mem", None),
        P("band", "mem", None),
    )
    return jax.shard_map(
        local,
        mesh=mesh,
        in_specs=placed,
        out_specs=(P("mem", "band", None), P("band", "mem", None, None)),
        check_vma=False,
    )
```

```python
import functools
import math

import jax
import jax.numpy as jnp
from jax import lax
from jax.experimental import pallas as pl
from jax.experimental.pallas import tpu as pltpu
from jax.sharding import PartitionSpec as P

C0, C1, C2, C3, C4 = 2.25, -2.4375, 1.6875, -0.5625, 0.0625
PAIRS = 6
MESH = pl.DeviceIdType.MESH
HIGHEST = lax.Precision.HIGHEST


def whole():
    return pl.BlockSpec(memory_space=pltpu.VMEM)


def pieces(x):
    high = x.astype(jnp.bfloat16)
    return high, (x - high.astype(jnp.float32)).astype(jnp.bfloat16)


def product(left, right, right_dim=0):
    lh, ll = left
    rh, rl = right
    return lax.dot_general(
        jnp.concatenate([lh, lh, ll], axis=1),
        jnp.concatenate([rh, rl, rh], axis=right_dim),
        (((1,), (right_dim,)), ((), ())),
        preferred_element_type=jnp.float32,
    )


def exact(left, right, right_dim=0):
    return lax.dot_general(
        left, right, (((1,), (right_dim,)), ((), ())),
        precision=HIGHEST, preferred_element_type=jnp.float32,
    )


def pair_change(m):
    mp = pieces(m)
    square = product(mp, mp)
    return (C1 * m + C2 * square) + product(pieces(square), pieces(C3 * m + C4 * square))


def apply_twice(factor, column):
    row = jnp.sum(factor * column, axis=0, keepdims=True)
    return jnp.sum(factor * row, axis=1, keepdims=True)


def pair_step(y_ref, z_ref, col_ref, diagonal, group, last):
    for g in range(group):
        y, z = y_ref[g], z_ref[g]
        yp, zp = pieces(y), pieces(z)
        change = pair_change(product(zp, yp))
        parts = pieces(change)
        if not last:
            y_ref[g] = C0 * y + product(yp, parts)
        z_ref[g] = C0 * z + product(parts, zp)
        col_ref[g] = apply_twice(change + diagonal, col_ref[g])


def partner(me, d, n_mem):
    return lax.rem(me + d + 1, n_mem)


def analyse(n_mem, group, order_hbm, count_hbm, x_hbm, op_hbm, index_hbm, value_hbm, weight_hbm, spread_out, back_ref,
            order_ref, count_ref, op_ref, index_ref, value_ref, weight_ref, spread_ref,
            lanes_ref, sends_ref, inbox, outbox, pert_ref, y_ref, z_ref, col_ref, mean_ref,
            load_sem, lane_sem, spread_sem, in_send, in_recv, own_sem, out_send, out_recv, home_sem):
    per_worker, workers, rows_dev, cells = inbox.shape
    members = workers * rows_dev
    levels = op_ref.shape[0]
    slots = index_ref.shape[1]
    me = lax.axis_index("mem")
    halves, _, lanes = lanes_ref.shape
    band = order_ref.shape[0]
    barrier = pltpu.get_barrier_semaphore()

    order_load = pltpu.make_async_copy(order_hbm, order_ref, load_sem.at[0])
    order_load.start()
    lane_loads = [
        pltpu.make_async_copy(x_hbm.at[:, pl.ds(h * lanes, lanes)], lanes_ref.at[h], lane_sem.at[h])
        for h in range(halves)
    ]
    for load in lane_loads:
        load.start()

    def greet(d, carry):
        pl.semaphore_signal(barrier, inc=1, device_id={"mem": partner(me, d, n_mem)}, device_id_type=MESH)
        return carry

    lax.fori_loop(0, n_mem - 1, greet, 0)
    mine = pl.ds(pl.multiple_of(me * per_worker, per_worker), per_worker)
    loads = [
        pltpu.make_async_copy(source, target, load_sem.at[1 + n])
        for n, (source, target) in enumerate([
            (count_hbm, count_ref), (op_hbm, op_ref), (index_hbm.at[mine], index_ref),
            (value_hbm, value_ref), (weight_hbm, weight_ref),
        ])
    ]
    for load in loads:
        load.start()
    order_load.wait()
    for load in lane_loads:
        load.wait()

    def stage(i):
        def one(w, carry):
            q = order_ref[w * per_worker + i]
            for h in range(halves):
                sends_ref[w, i, :, h * lanes:(h + 1) * lanes] = lanes_ref[h, pl.ds(q, rows_dev, stride=band), :]
            return carry

        lax.fori_loop(0, n_mem, one, 0)

    stage(0)
    pl.semaphore_wait(barrier, n_mem - 1)

    def keep(i):
        return pltpu.make_async_copy(spread_ref.at[i], spread_out.at[i], spread_sem.at[i])

    def own_in(i):
        return pltpu.make_async_copy(sends_ref.at[me, i], inbox.at[i, me], own_sem.at[i])

    def own_back(i):
        return pltpu.make_async_copy(outbox.at[i, me], back_ref.at[me, i], home_sem.at[i])

    def issue(i):
        own_in(i).start()

        def one(d, carry):
            peer = partner(me, d, n_mem)
            pltpu.make_async_remote_copy(
                src_ref=sends_ref.at[peer, i], dst_ref=inbox.at[i, me],
                send_sem=in_send, recv_sem=in_recv.at[i],
                device_id={"mem": peer}, device_id_type=MESH,
            ).start()
            return carry

        lax.fori_loop(0, n_mem - 1, one, 0)

    def feed(i, carry):
        stage(i)
        issue(i)
        return carry

    issue(0)
    lax.fori_loop(1, per_worker, feed, 0)
    for load in loads:
        load.wait()
    eye = (
        lax.broadcasted_iota(jnp.int32, (members, members), 0)
        == lax.broadcasted_iota(jnp.int32, (members, members), 1)
    )

    def run(base, size):
        for g in range(size):
            own_in(base + g).wait()
            arrived = inbox.at[base + g, pl.ds(0, n_mem - 1)]
            pltpu.make_async_copy(arrived, arrived, in_recv.at[base + g]).wait()
        scales = [prepare(base + g, g) for g in range(size)]

        for k in range(1, PAIRS):
            pair_step(y_ref, z_ref, col_ref, diagonal, size, k == PAIRS - 1)
        for g in range(size):
            finish(base + g, g, scales[g])
            launch(base + g)

    def launch(spot):
        own_back(spot).start()

        def one(d, carry):
            peer = partner(me, d, n_mem)
            pltpu.make_async_remote_copy(
                src_ref=outbox.at[spot, peer], dst_ref=back_ref.at[me, spot],
                send_sem=out_send, recv_sem=out_recv,
                device_id={"mem": peer}, device_id_type=MESH,
            ).start()
            return carry

        lax.fori_loop(0, n_mem - 1, one, 0)

    def prepare(spot, g):
        state = inbox[spot].reshape(members, cells)
        mean = jnp.mean(state, axis=0, keepdims=True)
        pert = state - mean
        pert_ref[g] = pert
        op = op_ref[...]
        columns = cells // levels
        op_pieces = pieces(op)
        chan = jnp.concatenate([product(pieces(pert[:, c * levels:(c + 1) * levels]), op_pieces) for c in range(columns)], axis=1)
        wide = jnp.broadcast_to(mean, (8, cells))
        chan_mean = jnp.concatenate([exact(wide[:, c * levels:(c + 1) * levels], op) for c in range(columns)], axis=1)
        width = chan.shape[1]
        index = index_ref[pl.ds(spot, 1), :]
        live = lax.broadcasted_iota(jnp.int32, (1, slots), 1) < count_ref[spot]
        weight = jnp.where(live, weight_ref[pl.ds(spot, 1), :], 0.0)
        value = weight * value_ref[pl.ds(spot, 1), :]
        picker = (lax.broadcasted_iota(jnp.int32, (width, slots), 0) == index).astype(jnp.bfloat16)
        sub = lax.broadcasted_iota(jnp.int32, (16, slots), 0)
        stack = jnp.where(sub == 0, weight, jnp.where(sub == 1, value, 0.0))
        s0 = stack.astype(jnp.bfloat16)
        left = stack - s0.astype(jnp.float32)
        s1 = left.astype(jnp.bfloat16)
        s2 = (left - s1.astype(jnp.float32)).astype(jnp.bfloat16)
        binned = lax.dot_general(
            jnp.concatenate([s0, s1, s2], axis=0), picker, (((1,), (1,)), ((), ())),
            preferred_element_type=jnp.float32,
        )
        binned = binned[0:16] + (binned[16:32] + binned[32:48])
        total = binned[0:1]
        innov = binned[1:2] - chan_mean[0:1] * total
        system = exact(chan * total, chan, 1) + jnp.where(eye, members - 1.0, 0.0)
        column = jnp.sum(chan * innov, axis=1, keepdims=True)
        mean_ref[g] = wide
        trace_value = jnp.sum(jnp.sum(jnp.where(eye, system, 0.0), axis=0, keepdims=True), axis=1, keepdims=True)
        y = system / trace_value
        change = pair_change(y)
        factor = change + diagonal
        z_ref[g] = factor
        y_ref[g] = C0 * y + product(pieces(y), pieces(change))
        col_ref[g] = apply_twice(factor, column)
        return trace_value

    def finish(spot, g, trace_value):
        z = z_ref[g]
        spread = z * (math.sqrt(members - 1.0) / jnp.sqrt(trace_value))
        spread_ref[spot] = spread
        keep(spot).start()
        weights = col_ref[g] / trace_value
        pert = pert_ref[g]
        shift = mean_ref[g][0:1] + jnp.sum(pert * weights, axis=0, keepdims=True)
        update = shift + product(pieces(spread), pieces(pert))
        outbox[spot] = update.reshape(workers, rows_dev, cells)

    diagonal = jnp.where(eye, C0, 0.0)

    edge = 1 if group > 1 and per_worker % group == 0 and per_worker > group else 0
    middle = (per_worker - 2 * edge) // group

    def step(t, carry):
        run(edge + t * group, group)
        return carry

    if edge:
        run(0, 1)
    lax.fori_loop(0, middle, step, 0)
    if edge:
        run(per_worker - 1, 1)
    sent = sends_ref.at[pl.ds(0, n_mem - 1)]
    pltpu.make_async_copy(sent, sent, in_send).wait()
    posted = back_ref.at[pl.ds(0, n_mem - 1)]
    pltpu.make_async_copy(posted, posted, out_send).wait()
    pltpu.make_async_copy(posted, posted, out_recv).wait()
    for i in range(per_worker):
        own_back(i).wait()
        keep(i).wait()


def restore(order_hbm, back, spread, out, spread_out, order_ref, order_sem, spread_sem, sem):
    n_mem, per_worker = back.shape[:2]
    load = pltpu.make_async_copy(order_hbm, order_ref, order_sem)
    load.start()
    passed = pltpu.make_async_copy(spread, spread_out, spread_sem)
    passed.start()
    load.wait()

    def place(t, carry):
        pltpu.make_async_copy(
            back.at[t // per_worker, lax.rem(t, per_worker)], out.at[:, order_ref[t], :], sem
        ).start()
        return carry

    lax.fori_loop(0, n_mem * per_worker, place, 0, unroll=8)
    pltpu.make_async_copy(out, out, sem).wait()
    passed.wait()


def local(ensemble, column_operator, patch_order, obs_index, obs_count, obs_values, obs_precision):
    rows_dev, band, cells = ensemble.shape
    slots = obs_index.shape[2]
    n_mem = lax.axis_size("mem")
    per_worker = band // n_mem
    members = rows_dev * n_mem
    group = 2 if per_worker % 2 == 0 else 1
    order = patch_order[0]
    held = pl.BlockSpec(memory_space=pltpu.HBM)
    free = pl.BlockSpec(memory_space=pl.ANY)
    block = jax.ShapeDtypeStruct((n_mem, per_worker, rows_dev, cells), jnp.float32)
    squares = jax.ShapeDtypeStruct((per_worker, members, members), jnp.float32)

    spread, back = pl.pallas_call(
        functools.partial(analyse, n_mem, group),
        out_shape=[squares, block],
        in_specs=[held] * 7,
        out_specs=[free, free],
        scratch_shapes=[
            pltpu.SMEM((band,), jnp.int32),
            pltpu.SMEM((per_worker,), jnp.int32),
            pltpu.VMEM(column_operator.shape, jnp.float32),
            pltpu.VMEM((per_worker, slots), jnp.int32),
            pltpu.VMEM((per_worker, slots), jnp.float32),
            pltpu.VMEM((per_worker, slots), jnp.float32),
            pltpu.VMEM((per_worker, members, members), jnp.float32),
            pltpu.VMEM((cells // 128, rows_dev * band, 128), jnp.float32),
            pltpu.VMEM((n_mem, per_worker, rows_dev, cells), jnp.float32),
            pltpu.VMEM((per_worker, n_mem, rows_dev, cells), jnp.float32),
            pltpu.VMEM((per_worker, n_mem, rows_dev, cells), jnp.float32),
            pltpu.VMEM((group, members, cells), jnp.float32),
            pltpu.VMEM((group, members, members), jnp.float32),
            pltpu.VMEM((group, members, members), jnp.float32),
            pltpu.VMEM((group, members, 1), jnp.float32),
            pltpu.VMEM((group, 8, cells), jnp.float32),
            pltpu.SemaphoreType.DMA((6,)),
            pltpu.SemaphoreType.DMA((cells // 128,)),
            pltpu.SemaphoreType.DMA((per_worker,)),
            pltpu.SemaphoreType.DMA(()),
            pltpu.SemaphoreType.DMA((per_worker,)),
            pltpu.SemaphoreType.DMA((per_worker,)),
            pltpu.SemaphoreType.DMA(()),
            pltpu.SemaphoreType.DMA(()),
            pltpu.SemaphoreType.DMA((per_worker,)),
        ],
        compiler_params=pltpu.CompilerParams(collective_id=0, has_side_effects=True, vmem_limit_bytes=40 << 20),
        name="analyse",
    )(*[pltpu.with_memory_space_constraint(part, pltpu.HBM) for part in (order, obs_count[0], ensemble.reshape(rows_dev * band, cells), column_operator, obs_index[0], obs_values[0], obs_precision[0])])

    restored, transform = pl.pallas_call(
        restore,
        out_shape=[jax.ShapeDtypeStruct((rows_dev, band, cells), jnp.float32), squares],
        in_specs=[held, free, free],
        out_specs=[held, held],
        scratch_shapes=[
            pltpu.SMEM((band,), jnp.int32),
            pltpu.SemaphoreType.DMA(()),
            pltpu.SemaphoreType.DMA(()),
            pltpu.SemaphoreType.DMA(()),
        ],
        compiler_params=pltpu.CompilerParams(vmem_limit_bytes=16 << 20),
        name="restore_patches",
    )(order, back, spread)
    return (restored, transform[None])


def solution(mesh):
    placed = (
        P("mem", "band", None),
        P(),
        P("band", None),
        P("band", None, None),
        P("band", "mem"),
        P("band", "mem", None),
        P("band", "mem", None),
    )
    return jax.shard_map(
        local,
        mesh=mesh,
        in_specs=placed,
        out_specs=(P("mem", "band", None), P("band", "mem", None, None)),
        check_vma=False,
    )
```

```python
import functools
import math

import jax
import jax.numpy as jnp
from jax import lax
from jax.experimental import pallas as pl
from jax.experimental.pallas import tpu as pltpu
from jax.sharding import PartitionSpec as P

C0, C1, C2, C3, C4 = 2.25, -2.4375, 1.6875, -0.5625, 0.0625
PAIRS = 6
MESH = pl.DeviceIdType.MESH
HIGHEST = lax.Precision.HIGHEST


def whole():
    return pl.BlockSpec(memory_space=pltpu.VMEM)


def pieces(x):
    high = x.astype(jnp.bfloat16)
    return high, (x - high.astype(jnp.float32)).astype(jnp.bfloat16)


def product(left, right, right_dim=0):
    lh, ll = left
    rh, rl = right
    return lax.dot_general(
        jnp.concatenate([lh, lh, ll], axis=1),
        jnp.concatenate([rh, rl, rh], axis=right_dim),
        (((1,), (right_dim,)), ((), ())),
        preferred_element_type=jnp.float32,
    )


def exact(left, right, right_dim=0):
    return lax.dot_general(
        left, right, (((1,), (right_dim,)), ((), ())),
        precision=HIGHEST, preferred_element_type=jnp.float32,
    )


def pair_change(m):
    mp = pieces(m)
    square = product(mp, mp)
    return (C1 * m + C2 * square) + product(pieces(square), pieces(C3 * m + C4 * square))


def apply_twice(factor, column):
    row = jnp.sum(factor * column, axis=0, keepdims=True)
    return jnp.sum(factor * row, axis=1, keepdims=True)


def pair_step(y_ref, z_ref, col_ref, diagonal, group, last):
    span = range(group)
    y = [y_ref[g] for g in span]
    z = [z_ref[g] for g in span]
    yp = [pieces(part) for part in y]
    zp = [pieces(part) for part in z]
    m = [product(zp[g], yp[g]) for g in span]
    mp = [pieces(part) for part in m]
    square = [product(mp[g], mp[g]) for g in span]
    rest = [pieces(C3 * m[g] + C4 * square[g]) for g in span]
    change = [(C1 * m[g] + C2 * square[g]) + product(pieces(square[g]), rest[g]) for g in span]
    parts = [pieces(part) for part in change]
    for g in span:
        if not last:
            y_ref[g] = C0 * y[g] + product(yp[g], parts[g])
        z_ref[g] = C0 * z[g] + product(parts[g], zp[g])
    for g in span:
        col_ref[g] = apply_twice(change[g] + diagonal, col_ref[g])


def partner(me, d, n_mem):
    return lax.rem(me + d + 1, n_mem)


def analyse(n_mem, group, order_hbm, count_hbm, x_hbm, op_hbm, index_hbm, value_hbm, weight_hbm, spread_out, back_ref,
            order_ref, count_ref, op_ref, index_ref, value_ref, weight_ref, spread_ref,
            lanes_ref, sends_ref, inbox, outbox, pert_ref, y_ref, z_ref, col_ref, mean_ref,
            load_sem, lane_sem, spread_sem, in_send, in_recv, own_sem, out_send, out_recv, home_sem):
    per_worker, workers, rows_dev, cells = inbox.shape
    members = workers * rows_dev
    levels = op_ref.shape[0]
    slots = index_ref.shape[1]
    me = lax.axis_index("mem")
    halves, _, lanes = lanes_ref.shape
    band = order_ref.shape[0]
    barrier = pltpu.get_barrier_semaphore()

    order_load = pltpu.make_async_copy(order_hbm, order_ref, load_sem.at[0])
    order_load.start()
    lane_loads = [
        pltpu.make_async_copy(x_hbm.at[:, pl.ds(h * lanes, lanes)], lanes_ref.at[h], lane_sem.at[h])
        for h in range(halves)
    ]
    for load in lane_loads:
        load.start()

    def greet(d, carry):
        pl.semaphore_signal(barrier, inc=1, device_id={"mem": partner(me, d, n_mem)}, device_id_type=MESH)
        return carry

    lax.fori_loop(0, n_mem - 1, greet, 0)
    mine = pl.ds(pl.multiple_of(me * per_worker, per_worker), per_worker)
    loads = [
        pltpu.make_async_copy(source, target, load_sem.at[1 + n])
        for n, (source, target) in enumerate([
            (count_hbm, count_ref), (op_hbm, op_ref), (index_hbm.at[mine], index_ref),
            (value_hbm, value_ref), (weight_hbm, weight_ref),
        ])
    ]
    for load in loads:
        load.start()
    order_load.wait()
    for load in lane_loads:
        load.wait()

    def stage(i):
        def one(w, carry):
            q = order_ref[w * per_worker + i]
            for h in range(halves):
                sends_ref[w, i, :, h * lanes:(h + 1) * lanes] = lanes_ref[h, pl.ds(q, rows_dev, stride=band), :]
            return carry

        lax.fori_loop(0, n_mem, one, 0)

    stage(0)
    pl.semaphore_wait(barrier, n_mem - 1)

    def keep(i):
        return pltpu.make_async_copy(spread_ref.at[i], spread_out.at[i], spread_sem.at[i])

    def own_in(i):
        return pltpu.make_async_copy(sends_ref.at[me, i], inbox.at[i, me], own_sem.at[i])

    def own_back(i):
        return pltpu.make_async_copy(outbox.at[i, me], back_ref.at[me, i], home_sem.at[i])

    def issue(i):
        own_in(i).start()

        def one(d, carry):
            peer = partner(me, d, n_mem)
            pltpu.make_async_remote_copy(
                src_ref=sends_ref.at[peer, i], dst_ref=inbox.at[i, me],
                send_sem=in_send, recv_sem=in_recv.at[i],
                device_id={"mem": peer}, device_id_type=MESH,
            ).start()
            return carry

        lax.fori_loop(0, n_mem - 1, one, 0)

    def feed(i, carry):
        stage(i)
        issue(i)
        return carry

    issue(0)
    lax.fori_loop(1, per_worker, feed, 0)
    for load in loads:
        load.wait()
    eye = (
        lax.broadcasted_iota(jnp.int32, (members, members), 0)
        == lax.broadcasted_iota(jnp.int32, (members, members), 1)
    )

    def run(base, size):
        for g in range(size):
            own_in(base + g).wait()
            arrived = inbox.at[base + g, pl.ds(0, n_mem - 1)]
            pltpu.make_async_copy(arrived, arrived, in_recv.at[base + g]).wait()
        scales = [prepare(base + g, g) for g in range(size)]

        for k in range(1, PAIRS):
            pair_step(y_ref, z_ref, col_ref, diagonal, size, k == PAIRS - 1)
        for g in range(size):
            finish(base + g, g, scales[g])
            launch(base + g)

    def launch(spot):
        own_back(spot).start()

        def one(d, carry):
            peer = partner(me, d, n_mem)
            pltpu.make_async_remote_copy(
                src_ref=outbox.at[spot, peer], dst_ref=back_ref.at[me, spot],
                send_sem=out_send, recv_sem=out_recv,
                device_id={"mem": peer}, device_id_type=MESH,
            ).start()
            return carry

        lax.fori_loop(0, n_mem - 1, one, 0)

    def prepare(spot, g):
        state = inbox[spot].reshape(members, cells)
        mean = jnp.mean(state, axis=0, keepdims=True)
        pert = state - mean
        pert_ref[g] = pert
        op = op_ref[...]
        columns = cells // levels
        op_pieces = pieces(op)
        chan = jnp.concatenate([product(pieces(pert[:, c * levels:(c + 1) * levels]), op_pieces) for c in range(columns)], axis=1)
        wide = jnp.broadcast_to(mean, (8, cells))
        chan_mean = jnp.concatenate([exact(wide[:, c * levels:(c + 1) * levels], op) for c in range(columns)], axis=1)
        width = chan.shape[1]
        index = index_ref[pl.ds(spot, 1), :]
        live = lax.broadcasted_iota(jnp.int32, (1, slots), 1) < count_ref[spot]
        weight = jnp.where(live, weight_ref[pl.ds(spot, 1), :], 0.0)
        value = weight * value_ref[pl.ds(spot, 1), :]
        picker = (lax.broadcasted_iota(jnp.int32, (width, slots), 0) == index).astype(jnp.bfloat16)
        sub = lax.broadcasted_iota(jnp.int32, (16, slots), 0)
        stack = jnp.where(sub == 0, weight, jnp.where(sub == 1, value, 0.0))
        s0 = stack.astype(jnp.bfloat16)
        left = stack - s0.astype(jnp.float32)
        s1 = left.astype(jnp.bfloat16)
        s2 = (left - s1.astype(jnp.float32)).astype(jnp.bfloat16)
        binned = lax.dot_general(
            jnp.concatenate([s0, s1, s2], axis=0), picker, (((1,), (1,)), ((), ())),
            preferred_element_type=jnp.float32,
        )
        binned = binned[0:16] + (binned[16:32] + binned[32:48])
        total = binned[0:1]
        innov = binned[1:2] - chan_mean[0:1] * total
        system = exact(chan * total, chan, 1) + jnp.where(eye, members - 1.0, 0.0)
        column = jnp.sum(chan * innov, axis=1, keepdims=True)
        mean_ref[g] = wide
        trace_value = jnp.sum(jnp.sum(jnp.where(eye, system, 0.0), axis=0, keepdims=True), axis=1, keepdims=True)
        y = system / trace_value
        change = pair_change(y)
        factor = change + diagonal
        z_ref[g] = factor
        y_ref[g] = C0 * y + product(pieces(y), pieces(change))
        col_ref[g] = apply_twice(factor, column)
        return trace_value

    def finish(spot, g, trace_value):
        z = z_ref[g]
        spread = z * (math.sqrt(members - 1.0) / jnp.sqrt(trace_value))
        spread_ref[spot] = spread
        keep(spot).start()
        weights = col_ref[g] / trace_value
        pert = pert_ref[g]
        shift = mean_ref[g][0:1] + jnp.sum(pert * weights, axis=0, keepdims=True)
        update = shift + product(pieces(spread), pieces(pert))
        outbox[spot] = update.reshape(workers, rows_dev, cells)

    diagonal = jnp.where(eye, C0, 0.0)

    edge = 1 if group > 1 and per_worker % group == 0 and per_worker > group else 0
    middle = (per_worker - 2 * edge) // group

    def step(t, carry):
        run(edge + t * group, group)
        return carry

    if edge:
        run(0, 1)
    lax.fori_loop(0, middle, step, 0)
    if edge:
        run(per_worker - 1, 1)
    sent = sends_ref.at[pl.ds(0, n_mem - 1)]
    pltpu.make_async_copy(sent, sent, in_send).wait()
    posted = back_ref.at[pl.ds(0, n_mem - 1)]
    pltpu.make_async_copy(posted, posted, out_send).wait()
    pltpu.make_async_copy(posted, posted, out_recv).wait()
    for i in range(per_worker):
        own_back(i).wait()
        keep(i).wait()


def restore(order_hbm, back, spread, out, spread_out, order_ref, order_sem, spread_sem, sem):
    n_mem, per_worker = back.shape[:2]
    load = pltpu.make_async_copy(order_hbm, order_ref, order_sem)
    load.start()
    passed = pltpu.make_async_copy(spread, spread_out, spread_sem)
    passed.start()
    load.wait()

    def place(t, carry):
        pltpu.make_async_copy(
            back.at[t // per_worker, lax.rem(t, per_worker)], out.at[:, order_ref[t], :], sem
        ).start()
        return carry

    lax.fori_loop(0, n_mem * per_worker, place, 0, unroll=8)
    pltpu.make_async_copy(out, out, sem).wait()
    passed.wait()


def local(ensemble, column_operator, patch_order, obs_index, obs_count, obs_values, obs_precision):
    rows_dev, band, cells = ensemble.shape
    slots = obs_index.shape[2]
    n_mem = lax.axis_size("mem")
    per_worker = band // n_mem
    members = rows_dev * n_mem
    group = 2 if per_worker % 2 == 0 else 1
    order = patch_order[0]
    held = pl.BlockSpec(memory_space=pltpu.HBM)
    free = pl.BlockSpec(memory_space=pl.ANY)
    block = jax.ShapeDtypeStruct((n_mem, per_worker, rows_dev, cells), jnp.float32)
    squares = jax.ShapeDtypeStruct((per_worker, members, members), jnp.float32)

    spread, back = pl.pallas_call(
        functools.partial(analyse, n_mem, group),
        out_shape=[squares, block],
        in_specs=[held] * 7,
        out_specs=[free, free],
        scratch_shapes=[
            pltpu.SMEM((band,), jnp.int32),
            pltpu.SMEM((per_worker,), jnp.int32),
            pltpu.VMEM(column_operator.shape, jnp.float32),
            pltpu.VMEM((per_worker, slots), jnp.int32),
            pltpu.VMEM((per_worker, slots), jnp.float32),
            pltpu.VMEM((per_worker, slots), jnp.float32),
            pltpu.VMEM((per_worker, members, members), jnp.float32),
            pltpu.VMEM((cells // 128, rows_dev * band, 128), jnp.float32),
            pltpu.VMEM((n_mem, per_worker, rows_dev, cells), jnp.float32),
            pltpu.VMEM((per_worker, n_mem, rows_dev, cells), jnp.float32),
            pltpu.VMEM((per_worker, n_mem, rows_dev, cells), jnp.float32),
            pltpu.VMEM((group, members, cells), jnp.float32),
            pltpu.VMEM((group, members, members), jnp.float32),
            pltpu.VMEM((group, members, members), jnp.float32),
            pltpu.VMEM((group, members, 1), jnp.float32),
            pltpu.VMEM((group, 8, cells), jnp.float32),
            pltpu.SemaphoreType.DMA((6,)),
            pltpu.SemaphoreType.DMA((cells // 128,)),
            pltpu.SemaphoreType.DMA((per_worker,)),
            pltpu.SemaphoreType.DMA(()),
            pltpu.SemaphoreType.DMA((per_worker,)),
            pltpu.SemaphoreType.DMA((per_worker,)),
            pltpu.SemaphoreType.DMA(()),
            pltpu.SemaphoreType.DMA(()),
            pltpu.SemaphoreType.DMA((per_worker,)),
        ],
        compiler_params=pltpu.CompilerParams(collective_id=0, has_side_effects=True, vmem_limit_bytes=40 << 20),
        name="analyse",
    )(*[pltpu.with_memory_space_constraint(part, pltpu.HBM) for part in (order, obs_count[0], ensemble.reshape(rows_dev * band, cells), column_operator, obs_index[0], obs_values[0], obs_precision[0])])

    restored, transform = pl.pallas_call(
        restore,
        out_shape=[jax.ShapeDtypeStruct((rows_dev, band, cells), jnp.float32), squares],
        in_specs=[held, free, free],
        out_specs=[held, held],
        scratch_shapes=[
            pltpu.SMEM((band,), jnp.int32),
            pltpu.SemaphoreType.DMA(()),
            pltpu.SemaphoreType.DMA(()),
            pltpu.SemaphoreType.DMA(()),
        ],
        compiler_params=pltpu.CompilerParams(vmem_limit_bytes=16 << 20),
        name="restore_patches",
    )(order, back, spread)
    return (restored, transform[None])


def solution(mesh):
    placed = (
        P("mem", "band", None),
        P(),
        P("band", None),
        P("band", None, None),
        P("band", "mem"),
        P("band", "mem", None),
        P("band", "mem", None),
    )
    return jax.shard_map(
        local,
        mesh=mesh,
        in_specs=placed,
        out_specs=(P("mem", "band", None), P("band", "mem", None, None)),
        check_vma=False,
    )
```

```python
import functools
import math

import jax
import jax.numpy as jnp
from jax import lax
from jax.experimental import pallas as pl
from jax.experimental.pallas import tpu as pltpu
from jax.sharding import PartitionSpec as P

C0, C1, C2, C3, C4 = 2.25, -2.4375, 1.6875, -0.5625, 0.0625
PAIRS = 6
MESH = pl.DeviceIdType.MESH
HIGHEST = lax.Precision.HIGHEST


def whole():
    return pl.BlockSpec(memory_space=pltpu.VMEM)


def pieces(x):
    high = x.astype(jnp.bfloat16)
    return high, (x - high.astype(jnp.float32)).astype(jnp.bfloat16)


def product(left, right, right_dim=0):
    lh, ll = left
    rh, rl = right
    return lax.dot_general(
        jnp.concatenate([lh, lh, ll], axis=1),
        jnp.concatenate([rh, rl, rh], axis=right_dim),
        (((1,), (right_dim,)), ((), ())),
        preferred_element_type=jnp.float32,
    )


def exact(left, right, right_dim=0):
    return lax.dot_general(
        left, right, (((1,), (right_dim,)), ((), ())),
        precision=HIGHEST, preferred_element_type=jnp.float32,
    )


def pair_change(m):
    mp = pieces(m)
    square = product(mp, mp)
    return (C1 * m + C2 * square) + product(pieces(square), pieces(C3 * m + C4 * square))


def apply_twice(factor, column):
    row = jnp.sum(factor * column, axis=0, keepdims=True)
    return jnp.sum(factor * row, axis=1, keepdims=True)


def pair_step(y_ref, z_ref, col_ref, diagonal, group, last):
    span = range(group)
    y = [y_ref[g] for g in span]
    z = [z_ref[g] for g in span]
    yp = [pieces(part) for part in y]
    zp = [pieces(part) for part in z]
    m = [product(zp[g], yp[g]) for g in span]
    mp = [pieces(part) for part in m]
    square = [product(mp[g], mp[g]) for g in span]
    rest = [pieces(C3 * m[g] + C4 * square[g]) for g in span]
    change = [(C1 * m[g] + C2 * square[g]) + product(pieces(square[g]), rest[g]) for g in span]
    parts = [pieces(part) for part in change]
    for g in span:
        if not last:
            y_ref[g] = C0 * y[g] + product(yp[g], parts[g])
        z_ref[g] = C0 * z[g] + product(parts[g], zp[g])
    for g in span:
        col_ref[g] = apply_twice(change[g] + diagonal, col_ref[g])


def partner(me, d, n_mem):
    return lax.rem(me + d + 1, n_mem)


def farthest(me, d, n_mem):
    high = n_mem - 1 - d
    return jnp.where(2 * me < n_mem, jnp.where(high > me, high, high - 1), jnp.where(d < me, d, d + 1))


def analyse(n_mem, group, order_hbm, count_hbm, x_hbm, op_hbm, index_hbm, value_hbm, weight_hbm, spread_out, back_ref,
            order_ref, count_ref, op_ref, index_ref, value_ref, weight_ref, spread_ref,
            lanes_ref, sends_ref, inbox, outbox, pert_ref, y_ref, z_ref, col_ref, mean_ref,
            load_sem, lane_sem, spread_sem, in_send, in_recv, own_sem, out_send, out_recv, home_sem):
    per_worker, workers, rows_dev, cells = inbox.shape
    members = workers * rows_dev
    levels = op_ref.shape[0]
    slots = index_ref.shape[1]
    me = lax.axis_index("mem")
    halves, _, lanes = lanes_ref.shape
    band = order_ref.shape[0]
    barrier = pltpu.get_barrier_semaphore()

    order_load = pltpu.make_async_copy(order_hbm, order_ref, load_sem.at[0])
    order_load.start()
    lane_loads = [
        pltpu.make_async_copy(x_hbm.at[:, pl.ds(h * lanes, lanes)], lanes_ref.at[h], lane_sem.at[h])
        for h in range(halves)
    ]
    for load in lane_loads:
        load.start()

    def greet(d, carry):
        pl.semaphore_signal(barrier, inc=1, device_id={"mem": farthest(me, d, n_mem)}, device_id_type=MESH)
        return carry

    lax.fori_loop(0, n_mem - 1, greet, 0)
    mine = pl.ds(pl.multiple_of(me * per_worker, per_worker), per_worker)
    loads = [
        pltpu.make_async_copy(source, target, load_sem.at[1 + n])
        for n, (source, target) in enumerate([
            (count_hbm, count_ref), (op_hbm, op_ref), (index_hbm.at[mine], index_ref),
            (value_hbm, value_ref), (weight_hbm, weight_ref),
        ])
    ]
    for load in loads:
        load.start()
    order_load.wait()
    for load in lane_loads:
        load.wait()

    def stage(i):
        def one(w, carry):
            q = order_ref[w * per_worker + i]
            for h in range(halves):
                sends_ref[w, i, :, h * lanes:(h + 1) * lanes] = lanes_ref[h, pl.ds(q, rows_dev, stride=band), :]
            return carry

        lax.fori_loop(0, n_mem, one, 0)

    stage(0)
    pl.semaphore_wait(barrier, n_mem - 1)

    def keep(i):
        return pltpu.make_async_copy(spread_ref.at[i], spread_out.at[i], spread_sem.at[i])

    def own_in(i):
        return pltpu.make_async_copy(sends_ref.at[me, i], inbox.at[i, me], own_sem.at[i])

    def own_back(i):
        return pltpu.make_async_copy(outbox.at[i, me], back_ref.at[me, i], home_sem.at[i])

    def issue(i):
        own_in(i).start()

        def one(d, carry):
            peer = farthest(me, d, n_mem)
            pltpu.make_async_remote_copy(
                src_ref=sends_ref.at[peer, i], dst_ref=inbox.at[i, me],
                send_sem=in_send, recv_sem=in_recv.at[i],
                device_id={"mem": peer}, device_id_type=MESH,
            ).start()
            return carry

        lax.fori_loop(0, n_mem - 1, one, 0)

    def feed(i, carry):
        stage(i)
        issue(i)
        return carry

    issue(0)
    lax.fori_loop(1, per_worker, feed, 0)
    for load in loads:
        load.wait()
    eye = (
        lax.broadcasted_iota(jnp.int32, (members, members), 0)
        == lax.broadcasted_iota(jnp.int32, (members, members), 1)
    )

    def run(base, size):
        for g in range(size):
            own_in(base + g).wait()
            arrived = inbox.at[base + g, pl.ds(0, n_mem - 1)]
            pltpu.make_async_copy(arrived, arrived, in_recv.at[base + g]).wait()
        scales = [prepare(base + g, g) for g in range(size)]

        for k in range(1, PAIRS):
            pair_step(y_ref, z_ref, col_ref, diagonal, size, k == PAIRS - 1)
        for g in range(size):
            finish(base + g, g, scales[g])
            launch(base + g)

    def launch(spot):
        own_back(spot).start()

        def one(d, carry):
            peer = farthest(me, d, n_mem)
            pltpu.make_async_remote_copy(
                src_ref=outbox.at[spot, peer], dst_ref=back_ref.at[me, spot],
                send_sem=out_send, recv_sem=out_recv,
                device_id={"mem": peer}, device_id_type=MESH,
            ).start()
            return carry

        lax.fori_loop(0, n_mem - 1, one, 0)

    def prepare(spot, g):
        state = inbox[spot].reshape(members, cells)
        mean = jnp.mean(state, axis=0, keepdims=True)
        pert = state - mean
        pert_ref[g] = pert
        op = op_ref[...]
        columns = cells // levels
        op_pieces = pieces(op)
        chan = jnp.concatenate([product(pieces(pert[:, c * levels:(c + 1) * levels]), op_pieces) for c in range(columns)], axis=1)
        wide = jnp.broadcast_to(mean, (8, cells))
        chan_mean = jnp.concatenate([exact(wide[:, c * levels:(c + 1) * levels], op) for c in range(columns)], axis=1)
        width = chan.shape[1]
        index = index_ref[pl.ds(spot, 1), :]
        live = lax.broadcasted_iota(jnp.int32, (1, slots), 1) < count_ref[spot]
        weight = jnp.where(live, weight_ref[pl.ds(spot, 1), :], 0.0)
        value = weight * value_ref[pl.ds(spot, 1), :]
        picker = (lax.broadcasted_iota(jnp.int32, (width, slots), 0) == index).astype(jnp.bfloat16)
        sub = lax.broadcasted_iota(jnp.int32, (16, slots), 0)
        stack = jnp.where(sub == 0, weight, jnp.where(sub == 1, value, 0.0))
        s0 = stack.astype(jnp.bfloat16)
        left = stack - s0.astype(jnp.float32)
        s1 = left.astype(jnp.bfloat16)
        s2 = (left - s1.astype(jnp.float32)).astype(jnp.bfloat16)
        binned = lax.dot_general(
            jnp.concatenate([s0, s1, s2], axis=0), picker, (((1,), (1,)), ((), ())),
            preferred_element_type=jnp.float32,
        )
        binned = binned[0:16] + (binned[16:32] + binned[32:48])
        total = binned[0:1]
        innov = binned[1:2] - chan_mean[0:1] * total
        system = exact(chan * total, chan, 1) + jnp.where(eye, members - 1.0, 0.0)
        column = jnp.sum(chan * innov, axis=1, keepdims=True)
        mean_ref[g] = wide
        trace_value = jnp.sum(jnp.sum(jnp.where(eye, system, 0.0), axis=0, keepdims=True), axis=1, keepdims=True)
        y = system / trace_value
        change = pair_change(y)
        factor = change + diagonal
        z_ref[g] = factor
        y_ref[g] = C0 * y + product(pieces(y), pieces(change))
        col_ref[g] = apply_twice(factor, column)
        return trace_value

    def finish(spot, g, trace_value):
        z = z_ref[g]
        spread = z * (math.sqrt(members - 1.0) / jnp.sqrt(trace_value))
        spread_ref[spot] = spread
        keep(spot).start()
        weights = col_ref[g] / trace_value
        pert = pert_ref[g]
        shift = mean_ref[g][0:1] + jnp.sum(pert * weights, axis=0, keepdims=True)
        update = shift + product(pieces(spread), pieces(pert))
        outbox[spot] = update.reshape(workers, rows_dev, cells)

    diagonal = jnp.where(eye, C0, 0.0)

    edge = 1 if group > 1 and per_worker % group == 0 and per_worker > group else 0
    middle = (per_worker - 2 * edge) // group

    def step(t, carry):
        run(edge + t * group, group)
        return carry

    if edge:
        run(0, 1)
    lax.fori_loop(0, middle, step, 0)
    if edge:
        run(per_worker - 1, 1)
    sent = sends_ref.at[pl.ds(0, n_mem - 1)]
    pltpu.make_async_copy(sent, sent, in_send).wait()
    posted = back_ref.at[pl.ds(0, n_mem - 1)]
    for i in range(per_worker):
        own_back(i).wait()
        keep(i).wait()
    pltpu.make_async_copy(posted, posted, out_send).wait()
    pltpu.make_async_copy(posted, posted, out_recv).wait()


def restore(order_hbm, back, spread, out, spread_out, order_ref, order_sem, spread_sem, sem):
    n_mem, per_worker = back.shape[:2]
    load = pltpu.make_async_copy(order_hbm, order_ref, order_sem)
    load.start()
    passed = pltpu.make_async_copy(spread, spread_out, spread_sem)
    passed.start()
    load.wait()

    def place(t, carry):
        pltpu.make_async_copy(
            back.at[t // per_worker, lax.rem(t, per_worker)], out.at[:, order_ref[t], :], sem
        ).start()
        return carry

    lax.fori_loop(0, n_mem * per_worker, place, 0, unroll=8)
    pltpu.make_async_copy(out, out, sem).wait()
    passed.wait()


def local(ensemble, column_operator, patch_order, obs_index, obs_count, obs_values, obs_precision):
    rows_dev, band, cells = ensemble.shape
    slots = obs_index.shape[2]
    n_mem = lax.axis_size("mem")
    per_worker = band // n_mem
    members = rows_dev * n_mem
    group = 2 if per_worker % 2 == 0 else 1
    order = patch_order[0]
    held = pl.BlockSpec(memory_space=pltpu.HBM)
    free = pl.BlockSpec(memory_space=pl.ANY)
    block = jax.ShapeDtypeStruct((n_mem, per_worker, rows_dev, cells), jnp.float32)
    squares = jax.ShapeDtypeStruct((per_worker, members, members), jnp.float32)

    spread, back = pl.pallas_call(
        functools.partial(analyse, n_mem, group),
        out_shape=[squares, block],
        in_specs=[held] * 7,
        out_specs=[free, free],
        scratch_shapes=[
            pltpu.SMEM((band,), jnp.int32),
            pltpu.SMEM((per_worker,), jnp.int32),
            pltpu.VMEM(column_operator.shape, jnp.float32),
            pltpu.VMEM((per_worker, slots), jnp.int32),
            pltpu.VMEM((per_worker, slots), jnp.float32),
            pltpu.VMEM((per_worker, slots), jnp.float32),
            pltpu.VMEM((per_worker, members, members), jnp.float32),
            pltpu.VMEM((cells // 128, rows_dev * band, 128), jnp.float32),
            pltpu.VMEM((n_mem, per_worker, rows_dev, cells), jnp.float32),
            pltpu.VMEM((per_worker, n_mem, rows_dev, cells), jnp.float32),
            pltpu.VMEM((per_worker, n_mem, rows_dev, cells), jnp.float32),
            pltpu.VMEM((group, members, cells), jnp.float32),
            pltpu.VMEM((group, members, members), jnp.float32),
            pltpu.VMEM((group, members, members), jnp.float32),
            pltpu.VMEM((group, members, 1), jnp.float32),
            pltpu.VMEM((group, 8, cells), jnp.float32),
            pltpu.SemaphoreType.DMA((6,)),
            pltpu.SemaphoreType.DMA((cells // 128,)),
            pltpu.SemaphoreType.DMA((per_worker,)),
            pltpu.SemaphoreType.DMA(()),
            pltpu.SemaphoreType.DMA((per_worker,)),
            pltpu.SemaphoreType.DMA((per_worker,)),
            pltpu.SemaphoreType.DMA(()),
            pltpu.SemaphoreType.DMA(()),
            pltpu.SemaphoreType.DMA((per_worker,)),
        ],
        compiler_params=pltpu.CompilerParams(collective_id=0, has_side_effects=True, vmem_limit_bytes=40 << 20),
        name="analyse",
    )(*[pltpu.with_memory_space_constraint(part, pltpu.HBM) for part in (order, obs_count[0], ensemble.reshape(rows_dev * band, cells), column_operator, obs_index[0], obs_values[0], obs_precision[0])])

    restored, transform = pl.pallas_call(
        restore,
        out_shape=[jax.ShapeDtypeStruct((rows_dev, band, cells), jnp.float32), squares],
        in_specs=[held, free, free],
        out_specs=[held, held],
        scratch_shapes=[
            pltpu.SMEM((band,), jnp.int32),
            pltpu.SemaphoreType.DMA(()),
            pltpu.SemaphoreType.DMA(()),
            pltpu.SemaphoreType.DMA(()),
        ],
        compiler_params=pltpu.CompilerParams(vmem_limit_bytes=16 << 20),
        name="restore_patches",
    )(order, back, spread)
    return (restored, transform[None])


def solution(mesh):
    placed = (
        P("mem", "band", None),
        P(),
        P("band", None),
        P("band", None, None),
        P("band", "mem"),
        P("band", "mem", None),
        P("band", "mem", None),
    )
    return jax.shard_map(
        local,
        mesh=mesh,
        in_specs=placed,
        out_specs=(P("mem", "band", None), P("band", "mem", None, None)),
        check_vma=False,
    )
```

```python
import functools
import math

import jax
import jax.numpy as jnp
from jax import lax
from jax.experimental import pallas as pl
from jax.experimental.pallas import tpu as pltpu
from jax.sharding import PartitionSpec as P

C0, C1, C2, C3, C4 = 2.25, -2.4375, 1.6875, -0.5625, 0.0625
PAIRS = 6
MESH = pl.DeviceIdType.MESH
HIGHEST = lax.Precision.HIGHEST


def whole():
    return pl.BlockSpec(memory_space=pltpu.VMEM)


def pieces(x):
    high = x.astype(jnp.bfloat16)
    return high, (x - high.astype(jnp.float32)).astype(jnp.bfloat16)


def product(left, right, right_dim=0):
    lh, ll = left
    rh, rl = right
    return lax.dot_general(
        jnp.concatenate([lh, lh, ll], axis=1),
        jnp.concatenate([rh, rl, rh], axis=right_dim),
        (((1,), (right_dim,)), ((), ())),
        preferred_element_type=jnp.float32,
    )


def exact(left, right, right_dim=0):
    return lax.dot_general(
        left, right, (((1,), (right_dim,)), ((), ())),
        precision=HIGHEST, preferred_element_type=jnp.float32,
    )


def pair_change(m):
    mp = pieces(m)
    square = product(mp, mp)
    return (C1 * m + C2 * square) + product(pieces(square), pieces(C3 * m + C4 * square))


def apply_twice(factor, column):
    row = jnp.sum(factor * column, axis=0, keepdims=True)
    return jnp.sum(factor * row, axis=1, keepdims=True)


def pair_step(y_ref, z_ref, col_ref, diagonal, group, last):
    span = range(group)
    y = [y_ref[g] for g in span]
    z = [z_ref[g] for g in span]
    yp = [pieces(part) for part in y]
    zp = [pieces(part) for part in z]
    m = [product(zp[g], yp[g]) for g in span]
    mp = [pieces(part) for part in m]
    square = [product(mp[g], mp[g]) for g in span]
    rest = [pieces(C3 * m[g] + C4 * square[g]) for g in span]
    change = [(C1 * m[g] + C2 * square[g]) + product(pieces(square[g]), rest[g]) for g in span]
    parts = [pieces(part) for part in change]
    for g in span:
        if not last:
            y_ref[g] = C0 * y[g] + product(yp[g], parts[g])
        z_ref[g] = C0 * z[g] + product(parts[g], zp[g])
    for g in span:
        col_ref[g] = apply_twice(change[g] + diagonal, col_ref[g])


def partner(me, d, n_mem):
    return lax.rem(me + d + 1, n_mem)


def farthest(me, d, n_mem):
    high = n_mem - 1 - d
    return jnp.where(2 * me < n_mem, jnp.where(high > me, high, high - 1), jnp.where(d < me, d, d + 1))


def analyse(n_mem, group, order_hbm, count_hbm, x_hbm, op_hbm, index_hbm, value_hbm, weight_hbm, spread_out, back_ref,
            order_ref, count_ref, op_ref, index_ref, value_ref, weight_ref, spread_ref,
            lanes_ref, sends_ref, inbox, outbox, pert_ref, y_ref, z_ref, col_ref, mean_ref,
            load_sem, lane_sem, spread_sem, in_send, in_recv, own_sem, out_send, out_recv, home_sem):
    per_worker, workers, rows_dev, cells = inbox.shape
    members = workers * rows_dev
    levels = op_ref.shape[0]
    slots = index_ref.shape[1]
    me = lax.axis_index("mem")
    halves, _, lanes = lanes_ref.shape
    band = order_ref.shape[0]
    barrier = pltpu.get_barrier_semaphore()

    order_load = pltpu.make_async_copy(order_hbm, order_ref, load_sem.at[0])
    order_load.start()
    lane_loads = [
        pltpu.make_async_copy(x_hbm.at[:, pl.ds(h * lanes, lanes)], lanes_ref.at[h], lane_sem.at[h])
        for h in range(halves)
    ]
    for load in lane_loads:
        load.start()

    def greet(d, carry):
        pl.semaphore_signal(barrier, inc=1, device_id={"mem": farthest(me, d, n_mem)}, device_id_type=MESH)
        return carry

    lax.fori_loop(0, n_mem - 1, greet, 0)
    mine = pl.ds(pl.multiple_of(me * per_worker, per_worker), per_worker)
    loads = [
        pltpu.make_async_copy(source, target, load_sem.at[1 + n])
        for n, (source, target) in enumerate([
            (count_hbm, count_ref), (op_hbm, op_ref), (index_hbm.at[mine], index_ref),
            (value_hbm, value_ref), (weight_hbm, weight_ref),
        ])
    ]
    for load in loads:
        load.start()
    order_load.wait()
    for load in lane_loads:
        load.wait()

    def stage(i):
        def one(w, carry):
            q = order_ref[w * per_worker + i]
            for h in range(halves):
                sends_ref[w, i, :, h * lanes:(h + 1) * lanes] = lanes_ref[h, pl.ds(q, rows_dev, stride=band), :]
            return carry

        lax.fori_loop(0, n_mem, one, 0)

    stage(0)
    pl.semaphore_wait(barrier, n_mem - 1)

    def keep(i):
        return pltpu.make_async_copy(spread_ref.at[i], spread_out.at[i], spread_sem.at[i])

    def own_in(i):
        return pltpu.make_async_copy(sends_ref.at[me, i], inbox.at[i, me], own_sem.at[i])

    def own_back(i):
        return pltpu.make_async_copy(outbox.at[i, me], back_ref.at[me, i], home_sem.at[i])

    def issue(i):
        own_in(i).start()

        def one(d, carry):
            peer = farthest(me, d, n_mem)
            pltpu.make_async_remote_copy(
                src_ref=sends_ref.at[peer, i], dst_ref=inbox.at[i, me],
                send_sem=in_send, recv_sem=in_recv.at[i],
                device_id={"mem": peer}, device_id_type=MESH,
            ).start()
            return carry

        lax.fori_loop(0, n_mem - 1, one, 0)

    def feed(i, carry):
        stage(i)
        issue(i)
        return carry

    issue(0)
    lax.fori_loop(1, per_worker, feed, 0)
    for load in loads:
        load.wait()
    eye = (
        lax.broadcasted_iota(jnp.int32, (members, members), 0)
        == lax.broadcasted_iota(jnp.int32, (members, members), 1)
    )

    def run(base, size):
        for g in range(size):
            own_in(base + g).wait()
            arrived = inbox.at[base + g, pl.ds(0, n_mem - 1)]
            pltpu.make_async_copy(arrived, arrived, in_recv.at[base + g]).wait()
        scales = [prepare(base + g, g) for g in range(size)]

        for k in range(1, PAIRS):
            pair_step(y_ref, z_ref, col_ref, diagonal, size, k == PAIRS - 1)
        for g in range(size):
            finish(base + g, g, scales[g])
            launch(base + g)

    def launch(spot):
        own_back(spot).start()

        def one(d, carry):
            peer = farthest(me, d, n_mem)
            pltpu.make_async_remote_copy(
                src_ref=outbox.at[spot, peer], dst_ref=back_ref.at[me, spot],
                send_sem=out_send, recv_sem=out_recv,
                device_id={"mem": peer}, device_id_type=MESH,
            ).start()
            return carry

        lax.fori_loop(0, n_mem - 1, one, 0)

    def prepare(spot, g):
        state = inbox[spot].reshape(members, cells)
        mean = jnp.mean(state, axis=0, keepdims=True)
        pert = state - mean
        pert_ref[g] = pert
        op = op_ref[...]
        columns = cells // levels
        op_pieces = pieces(op)
        chan = jnp.concatenate([product(pieces(pert[:, c * levels:(c + 1) * levels]), op_pieces) for c in range(columns)], axis=1)
        wide = jnp.broadcast_to(mean, (8, cells))
        chan_mean = jnp.concatenate([exact(wide[:, c * levels:(c + 1) * levels], op) for c in range(columns)], axis=1)
        width = chan.shape[1]
        index = index_ref[pl.ds(spot, 1), :]
        live = lax.broadcasted_iota(jnp.int32, (1, slots), 1) < count_ref[spot]
        weight = jnp.where(live, weight_ref[pl.ds(spot, 1), :], 0.0)
        value = weight * value_ref[pl.ds(spot, 1), :]
        picker = (lax.broadcasted_iota(jnp.int32, (width, slots), 0) == index).astype(jnp.bfloat16)
        sub = lax.broadcasted_iota(jnp.int32, (16, slots), 0)
        stack = jnp.where(sub == 0, weight, jnp.where(sub == 1, value, 0.0))
        s0 = stack.astype(jnp.bfloat16)
        left = stack - s0.astype(jnp.float32)
        s1 = left.astype(jnp.bfloat16)
        s2 = (left - s1.astype(jnp.float32)).astype(jnp.bfloat16)
        binned = lax.dot_general(
            jnp.concatenate([s0, s1, s2], axis=0), picker, (((1,), (1,)), ((), ())),
            preferred_element_type=jnp.float32,
        )
        binned = binned[0:16] + (binned[16:32] + binned[32:48])
        total = binned[0:1]
        innov = binned[1:2] - chan_mean[0:1] * total
        system = exact(chan * total, chan, 1) + jnp.where(eye, members - 1.0, 0.0)
        column = jnp.sum(chan * innov, axis=1, keepdims=True)
        mean_ref[g] = wide
        trace_value = jnp.sum(jnp.sum(jnp.where(eye, system, 0.0), axis=0, keepdims=True), axis=1, keepdims=True)
        y = system / trace_value
        change = pair_change(y)
        factor = change + diagonal
        z_ref[g] = factor
        y_ref[g] = C0 * y + product(pieces(y), pieces(change))
        col_ref[g] = apply_twice(factor, column)
        return trace_value

    def finish(spot, g, trace_value):
        z = z_ref[g]
        spread = z * (math.sqrt(members - 1.0) / jnp.sqrt(trace_value))
        spread_ref[spot] = spread
        keep(spot).start()
        weights = col_ref[g] / trace_value
        pert = pert_ref[g]
        shift = mean_ref[g][0:1] + jnp.sum(pert * weights, axis=0, keepdims=True)
        update = shift + product(pieces(spread), pieces(pert))
        outbox[spot] = update.reshape(workers, rows_dev, cells)

    diagonal = jnp.where(eye, C0, 0.0)

    edge = 1 if group > 1 and per_worker % group == 0 and per_worker > group else 0
    middle = (per_worker - 2 * edge) // group

    def step(t, carry):
        run(edge + t * group, group)
        return carry

    if edge:
        run(0, 1)
    lax.fori_loop(0, middle, step, 0)
    if edge:
        run(per_worker - 1, 1)
    sent = sends_ref.at[pl.ds(0, n_mem - 1)]
    pltpu.make_async_copy(sent, sent, in_send).wait()
    posted = back_ref.at[pl.ds(0, n_mem - 1)]
    for i in range(per_worker):
        own_back(i).wait()
        keep(i).wait()
    pltpu.make_async_copy(posted, posted, out_send).wait()
    pltpu.make_async_copy(posted, posted, out_recv).wait()


def restore(order_hbm, back, spread, out, spread_out, order_ref, order_sem, spread_sem, sem):
    n_mem, per_worker = back.shape[:2]
    load = pltpu.make_async_copy(order_hbm, order_ref, order_sem)
    load.start()
    passed = pltpu.make_async_copy(spread, spread_out, spread_sem)
    passed.start()
    load.wait()

    def place(t, carry):
        pltpu.make_async_copy(
            back.at[t // per_worker, lax.rem(t, per_worker)], out.at[:, order_ref[t], :], sem
        ).start()
        return carry

    lax.fori_loop(0, n_mem * per_worker, place, 0, unroll=64)
    pltpu.make_async_copy(out, out, sem).wait()
    passed.wait()


def local(ensemble, column_operator, patch_order, obs_index, obs_count, obs_values, obs_precision):
    rows_dev, band, cells = ensemble.shape
    slots = obs_index.shape[2]
    n_mem = lax.axis_size("mem")
    per_worker = band // n_mem
    members = rows_dev * n_mem
    group = 2 if per_worker % 2 == 0 else 1
    order = patch_order[0]
    held = pl.BlockSpec(memory_space=pltpu.HBM)
    free = pl.BlockSpec(memory_space=pl.ANY)
    block = jax.ShapeDtypeStruct((n_mem, per_worker, rows_dev, cells), jnp.float32)
    squares = jax.ShapeDtypeStruct((per_worker, members, members), jnp.float32)

    spread, back = pl.pallas_call(
        functools.partial(analyse, n_mem, group),
        out_shape=[squares, block],
        in_specs=[held] * 7,
        out_specs=[free, free],
        scratch_shapes=[
            pltpu.SMEM((band,), jnp.int32),
            pltpu.SMEM((per_worker,), jnp.int32),
            pltpu.VMEM(column_operator.shape, jnp.float32),
            pltpu.VMEM((per_worker, slots), jnp.int32),
            pltpu.VMEM((per_worker, slots), jnp.float32),
            pltpu.VMEM((per_worker, slots), jnp.float32),
            pltpu.VMEM((per_worker, members, members), jnp.float32),
            pltpu.VMEM((cells // 128, rows_dev * band, 128), jnp.float32),
            pltpu.VMEM((n_mem, per_worker, rows_dev, cells), jnp.float32),
            pltpu.VMEM((per_worker, n_mem, rows_dev, cells), jnp.float32),
            pltpu.VMEM((per_worker, n_mem, rows_dev, cells), jnp.float32),
            pltpu.VMEM((group, members, cells), jnp.float32),
            pltpu.VMEM((group, members, members), jnp.float32),
            pltpu.VMEM((group, members, members), jnp.float32),
            pltpu.VMEM((group, members, 1), jnp.float32),
            pltpu.VMEM((group, 8, cells), jnp.float32),
            pltpu.SemaphoreType.DMA((6,)),
            pltpu.SemaphoreType.DMA((cells // 128,)),
            pltpu.SemaphoreType.DMA((per_worker,)),
            pltpu.SemaphoreType.DMA(()),
            pltpu.SemaphoreType.DMA((per_worker,)),
            pltpu.SemaphoreType.DMA((per_worker,)),
            pltpu.SemaphoreType.DMA(()),
            pltpu.SemaphoreType.DMA(()),
            pltpu.SemaphoreType.DMA((per_worker,)),
        ],
        compiler_params=pltpu.CompilerParams(collective_id=0, has_side_effects=True, vmem_limit_bytes=40 << 20),
        name="analyse",
    )(*[pltpu.with_memory_space_constraint(part, pltpu.HBM) for part in (order, obs_count[0], ensemble.reshape(rows_dev * band, cells), column_operator, obs_index[0], obs_values[0], obs_precision[0])])

    restored, transform = pl.pallas_call(
        restore,
        out_shape=[jax.ShapeDtypeStruct((rows_dev, band, cells), jnp.float32), squares],
        in_specs=[held, free, free],
        out_specs=[held, held],
        scratch_shapes=[
            pltpu.SMEM((band,), jnp.int32),
            pltpu.SemaphoreType.DMA(()),
            pltpu.SemaphoreType.DMA(()),
            pltpu.SemaphoreType.DMA(()),
        ],
        compiler_params=pltpu.CompilerParams(vmem_limit_bytes=16 << 20),
        name="restore_patches",
    )(order, back, spread)
    return (restored, transform[None])


def solution(mesh):
    placed = (
        P("mem", "band", None),
        P(),
        P("band", None),
        P("band", None, None),
        P("band", "mem"),
        P("band", "mem", None),
        P("band", "mem", None),
    )
    return jax.shard_map(
        local,
        mesh=mesh,
        in_specs=placed,
        out_specs=(P("mem", "band", None), P("band", "mem", None, None)),
        check_vma=False,
    )
```
